32 devices in a mesh: leaf: 32 (over z, y, x, core).
Axes of the slice: x: 2, y: 2, z: 4, core: 2. Of those that a mesh axis runs over, the one named last changes fastest.
Arguments:
- points: bfloat16 [65536, 128], P('leaf'), may hold values from -6 to 6
- charges: bfloat16 [65536, 256], P('leaf'), may hold values from -6 to 6
- order: int32 [32, 2048], P('leaf'), may hold values from 0 to 2047, each once within a row
- near: int32 [32, 2], P('leaf'), may hold values from 0 to 31, as said below
- bases: bfloat16 [65536, 256], P('leaf'), may hold values from -0.125 to 0.125
- lift_leaf: float32 [8192, 256], P('leaf'), may hold values from -0.1875 to 0.1875
- lift_node: float32 [2048, 256], P('leaf'), may hold values from -0.1875 to 0.1875
- proxy_leaf: float32 [8192, 128], P('leaf'), may hold values from -5 to 5
- proxy_node: float32 [2048, 128], P('leaf'), may hold values from -5 to 5
- proxy_top: float32 [512, 128], P('leaf'), may hold values from -5 to 5
Outputs:
- potential: bfloat16 [65536, 256], P('leaf')
The draws below stay inside these ranges and needn't reach their ends.
Inputs may be any that keep to these rules, and one draw needn't show every extreme that they name: `order`: each row is a permutation of the leaf's 2048 positions. `near`: row l names two distinct leaves other than l from l's aligned group of four leaves; the relation is symmetric, and the group's remaining leaf is l's far partner, whose index differs from l in exactly one of the two lowest bits.
All inputs are finite; a program needn't handle non-finite values.
Results may differ from the reference program's by a relative error of at most 0.0049.
Values may be sent and summed in bfloat16 or wider, within the bound.
A program may use at most 64 MiB of HBM per device.

```python
import jax
import jax.numpy as jnp
from jax import lax

D = 128
NRHS = 256
RANK = 256
LEAF = 2048
NPTS = 65536
TOPN = 2
N_LEAF = 32


def draw_near(key, part):
    drawn_bits = jax.random.randint(key, (N_LEAF // 4,), 1, 3)
    group_ids = jnp.arange(N_LEAF // 4, dtype=jnp.int32)
    partner_bits = jnp.where(group_ids % 2 == 0, 2, drawn_bits).astype(jnp.int32)
    leaf_ids = jnp.arange(N_LEAF, dtype=jnp.int32)
    leaf_slot = leaf_ids % 4
    spread = jnp.repeat(partner_bits, 4).astype(jnp.int32)
    first_bits = jnp.where(spread == 1, 2, 1).astype(jnp.int32)
    second_bits = jnp.full((N_LEAF,), 3, jnp.int32)
    start = leaf_ids - leaf_slot
    first_near = start + jnp.bitwise_xor(leaf_slot, first_bits)
    second_near = start + jnp.bitwise_xor(leaf_slot, second_bits)
    return jnp.stack([first_near, second_near], axis=1).astype(jnp.int32)


def level_offset(key, salt):
    offset_key = jax.random.fold_in(key, salt)
    sign_key, size_key = jax.random.split(offset_key)
    signs = jnp.where(jax.random.bernoulli(sign_key, 0.5, (D,)), 1.0, -1.0).astype(jnp.float32)
    sizes = jax.random.uniform(size_key, (D,), jnp.float32, 0.45, 0.75)
    return signs * sizes


def normal_proxy(key, rows, salt):
    offset = level_offset(key, salt)
    noise = 0.75 * jax.random.normal(jax.random.fold_in(key, salt + 1), (rows, D), jnp.float32)
    return jnp.clip(offset[None, :] + noise, -5.0, 5.0).astype(jnp.float32)


def draw_proxy_leaf(key, part):
    return normal_proxy(key, N_LEAF * RANK, 101)


def draw_proxy_node(key, part):
    return normal_proxy(key, N_LEAF // 4 * RANK, 203)


def draw_proxy_top(key, part):
    return normal_proxy(key, TOPN * RANK, 307)


def steps_of(stream_key, dims, cuts, low, largest):
    loudness, own = 1.0, jax.random.fold_in(stream_key, 6)
    for dim, blocks in cuts:
        draws = jnp.exp(jax.random.uniform(jax.random.fold_in(own, dim), (blocks,), jnp.float32, low / len(cuts), largest / len(cuts)))
        loudness = loudness * jnp.repeat(draws, dims[dim] // blocks).reshape([-1 if axis == dim else 1 for axis in range(len(dims))])
    return loudness


def centred(key, shape, scale, most, cuts=(), held_as=jnp.bfloat16):
    values = scale * jax.random.normal(key, shape, jnp.float32)
    if cuts:
        values = values * steps_of(key, shape, cuts, -0.22, 0.18)
    return jnp.clip(values, -most, most).astype(held_as)


def setup_inputs(seed: int = 0) -> dict:
    streams_of = jax.random.split(jax.random.key(seed), 11)
    return {
        "points": centred(streams_of[0], (NPTS, D), 1.0, 6.0, ((0, 32),)),
        "charges": centred(streams_of[1], (NPTS, NRHS), 1.0, 6.0, ((0, 32),)),
        "order": jax.vmap(lambda own: jax.random.permutation(own, LEAF))(jax.random.split(streams_of[2], N_LEAF)).reshape((N_LEAF, LEAF)).astype(jnp.int32),
        "near": draw_near(jax.random.fold_in(streams_of[10], 71), 0),
        "bases": centred(streams_of[4], (NPTS, RANK), LEAF ** -0.5, 0.125, ((0, 32),)),
        "lift_leaf": centred(streams_of[5], (N_LEAF * RANK, RANK), (4 * RANK) ** -0.5, 0.1875, ((0, 32),), jnp.float32),
        "lift_node": centred(streams_of[6], (N_LEAF // 4 * RANK, RANK), (4 * RANK) ** -0.5, 0.1875, ((0, 32),), jnp.float32),
        "proxy_leaf": draw_proxy_leaf(jax.random.fold_in(streams_of[10], 71), 0),
        "proxy_node": draw_proxy_node(jax.random.fold_in(streams_of[10], 71), 0),
        "proxy_top": draw_proxy_top(jax.random.fold_in(streams_of[10], 71), 0),
    }


highest = lax.Precision.HIGHEST


def kernel_tile(left, right):
    products = jnp.dot(left, right.T, preferred_element_type=jnp.float32)
    left_norm = jnp.sum(jnp.square(left.astype(jnp.float32)), axis=1)
    right_norm = jnp.sum(jnp.square(right.astype(jnp.float32)), axis=1)
    return jnp.exp((2.0 * products - left_norm[:, None] - right_norm[None, :]) * (2.0 / D))


def couple(left, right):
    products = jnp.dot(left, right.T, precision=highest)
    left_norm = jnp.sum(left * left, axis=1)
    right_norm = jnp.sum(right * right, axis=1)
    return jnp.exp((2.0 * products - left_norm[:, None] - right_norm[None, :]) * (2.0 / D))


def reference(points, charges, order, near, bases, lift_leaf, lift_node, proxy_leaf, proxy_node, proxy_top):
    leaf_points = points.reshape(N_LEAF, LEAF, D)
    leaf_rhs = jnp.take_along_axis(charges.reshape(N_LEAF, LEAF, NRHS), order[:, :, None], axis=1)
    leaf_bases = bases.reshape(N_LEAF, LEAF, RANK)

    def near_leaf(leaf_id):
        total = jnp.zeros((LEAF, NRHS), jnp.float32)
        own = leaf_points[leaf_id]
        for source in (leaf_id, near[leaf_id, 0], near[leaf_id, 1]):
            tile = kernel_tile(own, leaf_points[source]).astype(jnp.bfloat16)
            total = total + jnp.dot(tile, leaf_rhs[source], preferred_element_type=jnp.float32)
        return total

    near_sum = lax.map(near_leaf, jnp.arange(N_LEAF, dtype=jnp.int32))

    def leaf_coeff(pair):
        return lax.dot_general(pair[0], pair[1], (((0,), (0,)), ((), ())), preferred_element_type=jnp.float32)

    coefficient = lax.map(leaf_coeff, (leaf_bases, leaf_rhs))
    lifts = lift_leaf.reshape(N_LEAF, RANK, RANK)
    upward = jnp.einsum("lkr,lkc->lrc", lifts, coefficient, precision=highest)
    node_coeff = upward.reshape(N_LEAF // 4, 4, RANK, NRHS).sum(axis=1)
    node_lifts = lift_node.reshape(N_LEAF // 4, RANK, RANK)
    top_coeff = jnp.einsum("gkr,gkc->grc", node_lifts, node_coeff, precision=highest)
    top_coeff = top_coeff.reshape(TOPN, 4, RANK, NRHS).sum(axis=1)
    leaf_proxy = proxy_leaf.reshape(N_LEAF, RANK, D)
    node_proxy = proxy_node.reshape(N_LEAF // 4, RANK, D)
    top_flat = top_coeff.reshape(TOPN * RANK, NRHS)
    owner = jnp.arange(TOPN * RANK, dtype=jnp.int32) // RANK

    def top_field(node):
        kernel = couple(lax.dynamic_slice_in_dim(proxy_top, node * RANK, RANK, 0), proxy_top)
        kernel = jnp.where(owner[None, :] != node, kernel, 0.0)
        return jnp.dot(kernel, top_flat, precision=highest)

    field_top = lax.map(top_field, jnp.arange(TOPN, dtype=jnp.int32))
    group_proxy = node_proxy.reshape(N_LEAF // 16, 4 * RANK, D)
    group_coeff = node_coeff.reshape(N_LEAF // 16, 4 * RANK, NRHS)
    sibling_owner = jnp.arange(4 * RANK, dtype=jnp.int32) // RANK

    def node_field(node):
        kernel = couple(node_proxy[node], group_proxy[node // 4])
        kernel = jnp.where(sibling_owner[None, :] != node % 4, kernel, 0.0)
        far_part = jnp.dot(kernel, group_coeff[node // 4], precision=highest)
        return far_part + jnp.dot(node_lifts[node], field_top[node // 4], precision=highest)

    field_node = lax.map(node_field, jnp.arange(N_LEAF // 4, dtype=jnp.int32))
    group_leaf_proxy = leaf_proxy.reshape(N_LEAF // 4, 4 * RANK, D)
    group_leaf_coeff = coefficient.reshape(N_LEAF // 4, 4 * RANK, NRHS)

    def leaf_field(leaf_id):
        partner = 6 - leaf_id % 4 - near[leaf_id, 0] % 4 - near[leaf_id, 1] % 4
        kernel = couple(leaf_proxy[leaf_id], group_leaf_proxy[leaf_id // 4])
        kernel = jnp.where(sibling_owner[None, :] == partner, kernel, 0.0)
        far_part = jnp.dot(kernel, group_leaf_coeff[leaf_id // 4], precision=highest)
        far_part = far_part + jnp.dot(lifts[leaf_id], field_node[leaf_id // 4], precision=highest)
        return far_part.astype(jnp.bfloat16)

    field_leaf = lax.map(leaf_field, jnp.arange(N_LEAF, dtype=jnp.int32))

    def descend(pair):
        return jnp.dot(pair[0], pair[1], preferred_element_type=jnp.float32)

    descent = lax.map(descend, (leaf_bases, field_leaf))
    return (near_sum + descent).astype(jnp.bfloat16).reshape(N_LEAF * LEAF, NRHS)
```

```python
import functools

import jax
import jax.numpy as jnp
from jax import lax
from jax.experimental import pallas as pl
from jax.experimental.pallas import tpu as pltpu
from jax.sharding import PartitionSpec as P

MESH = pl.DeviceIdType.MESH
F32, BF16 = jnp.float32, jnp.bfloat16
CHUNKS = 8
PARTS = 4
ROWS = 1024
VMEM_MB = 50


def mm(a, b, ca=1, cb=0):
    return lax.dot_general(a, b, (((ca,), (cb,)), ((), ())), preferred_element_type=F32)


def split3(x):
    high = x.astype(BF16).astype(F32)
    middle = (x - high).astype(BF16).astype(F32)
    return high, middle, x - high - middle


def norm_column(p):
    wide = p.astype(F32)
    return jnp.sum(wide * wide, axis=1, keepdims=True)


def norm_lanes(p, one_scale, norm_scale, norm_first):
    high, middle, low = split3(norm_column(p))
    lane = lax.broadcasted_iota(jnp.int32, (p.shape[0], 128), 1)
    first = 0 if norm_first else 3
    ones = jnp.where(lane < 6, one_scale, 0.0)
    out = jnp.where(lane == first, high * norm_scale, ones)
    out = jnp.where(lane == first + 1, middle * norm_scale, out)
    out = jnp.where(lane == first + 2, low * norm_scale, out)
    return out.astype(BF16)


def couple(left, right):
    scale = 2.0 / left.shape[1]
    wide = right.astype(F32)
    square = wide * wide
    high = square.astype(BF16)
    low = (square - high.astype(F32)).astype(BF16)
    ones = jnp.ones((8, left.shape[1]), BF16)
    right_norm = (mm(ones, high, 1, 1) + mm(ones, low, 1, 1))[0:1, :]
    return jnp.exp((2.0 * mm(left, right, 1, 1) - norm_column(left) - right_norm) * scale).astype(BF16)


def kernel(n, near, points_in, charges_in, bases_in, order, lift, nlift, zleaf, znode, ztop, out,
           points, charges, bases, rhs, rhst, laug, raug, acc, p1, p2, p3, r1, r2, r3, rmask, prel,
           t1, t2, saug, cr, racc, dsend, drecv, xsend, xrecv, fsend, frecv,
           c0, c0x, z0, z0x, ut, us, rs, nl, z1, z1s, z2, nv, nvs, c2, c2o, z2o, f1, f0,
           ssem, rsem, lsem):
    me = lax.axis_index("leaf")
    leaf, dim = points.shape
    rank = lift.shape[0]
    quarter = rank // 4
    sixteenth = rank // 16
    nodes = n // 16
    slot = me % 4
    group = me // 4 % 4
    part = me % 16
    node = me // 16
    step = leaf // CHUNKS
    wide = leaf // PARTS
    half = PARTS // 2
    blocks = leaf // ROWS
    gives = (me // 2 + me // 4) % 2 == 0
    works = (me // 2 + me // 4) % 2 == 1

    def flip(bits):
        where = me
        for bit in (1, 2, 4, 8):
            if bits & bit:
                where = where + bit - 2 * bit * (me // bit % 2)
        return where

    def flip_slot(bits):
        return flip(bits) % 4

    others = [(node + d) % nodes * 16 + part for d in range(1, nodes)]

    barrier = pltpu.get_barrier_semaphore()
    partners = [flip(b) for b in (1, 2, 4, 6, 8, 12)] + others
    for other in partners:
        pl.semaphore_signal(barrier, inc=1, device_id=(other,), device_id_type=MESH)

    loads = [pltpu.make_async_copy(a, b, lsem.at[i]) for i, (a, b) in enumerate(
        ((charges_in, charges), (bases_in, bases), (points_in, points)))]
    for copy in loads:
        copy.start()
    count = [0]

    def link(src, dst, device):
        i = count[0]
        count[0] += 1
        return pltpu.make_async_remote_copy(
            src_ref=src, dst_ref=dst, send_sem=ssem.at[i], recv_sem=rsem.at[i],
            device_id=(device,), device_id_type=MESH)

    started = []

    def send(src, dst, device):
        copy = link(src, dst, device)
        copy.start()
        started.append(copy)
        return copy

    def at_slot(bits):
        where = flip_slot(bits) if bits else slot
        return pl.ds(pl.multiple_of(where * quarter, quarter), quarter)

    mine = at_slot(0)
    mine16 = pl.ds(pl.multiple_of(part * sixteenth, sixteenth), sixteenth)
    far16 = pl.ds(pl.multiple_of(flip(2) % 16 * sixteenth, sixteenth), sixteenth)
    mine64 = pl.ds(pl.multiple_of(group * quarter, quarter), quarter)
    part_rows = [pl.ds(k * wide, wide) for k in range(PARTS)]
    step_rows = [pl.ds(j * step, step) for j in range(CHUNKS)]

    give_points = [link(points_in.at[r, :], p2.at[r, :], flip(2)) for r in part_rows[:half]]
    give_detour = [link(points_in.at[r, :], prel.at[pl.ds(k * wide, wide), :], flip(4))
                   for k, r in enumerate(part_rows[half:])]
    detour_on = [link(prel.at[pl.ds(k * wide, wide), :], p2.at[r, :], flip(6))
                 for k, r in enumerate(part_rows[half:])]
    give_proxy = link(z0, z0x.at[1], flip(2))
    give_coeff = link(c0, c0x.at[1], flip(2))
    give_rhs = [link(rhs.at[r, :], r2.at[r, :], flip(2)) for r in step_rows]
    share_points = [link(p2.at[r, :], p3.at[r, :], flip(1)) for r in part_rows]
    share_rhs = [link(r2.at[r, :], r3.at[r, :], flip(1)) for r in step_rows]
    cross_part = [link(dsend.at[k], drecv.at[k], flip(1)) for k in range(PARTS)]
    back_part = [link(xsend.at[k], xrecv.at[k], flip(2)) for k in range(PARTS)]
    back_far = link(fsend, frecv, flip(2))
    mate_rhs = link(rhs, r1, flip(1))
    up_two = link(us, rs.at[2], flip(2))
    phase_b = []
    for i, b in enumerate((4, 8, 12)):
        phase_b.append(link(z1, z1s.at[i], flip(b)))
        phase_b.append(link(z2.at[mine64, :], z2.at[mine64, :], flip(b)))
    phase_two = [link(nv, nvs.at[i], flip(b)) for i, b in enumerate((4, 8, 12))]
    phase_top = []
    for d, other in enumerate(others):
        phase_top.append(link(c2, c2o.at[d], other))
        phase_top.append(link(z2, z2o.at[d], other))
    down_two = link(f1.at[mine, :], f1.at[mine, :], flip(2))
    down_one = link(f1.at[mine, :], f1.at[mine, :], flip(1))
    down_rest = link(f1.at[at_slot(2), :], f1.at[at_slot(2), :], flip(1))

    z1[mine, :] = znode[...].astype(BF16)
    nl[mine, :] = nlift[...].astype(BF16)
    z2[mine16, :] = ztop[...].astype(BF16)
    z0[...] = zleaf[...].astype(BF16)
    pl.semaphore_wait(barrier, len(partners))

    phase_a2 = [send(z1.at[mine, :], z1.at[mine, :], flip(2)),
                send(nl.at[mine, :], nl.at[mine, :], flip(2)),
                send(z2.at[mine16, :], z2.at[mine16, :], flip(2))]

    @pl.when(gives)
    def _():
        for copy in give_points + give_detour + [give_proxy]:
            copy.start()

    phase_a = [send(z1.at[mine, :], z1.at[mine, :], flip(1)),
               send(nl.at[mine, :], nl.at[mine, :], flip(1)),
               send(z2.at[mine16, :], z2.at[mine16, :], flip(1))]
    mate_points = send(points_in, p1, flip(1))
    loads[0].wait()

    def permute(block, carry):
        rows = pl.ds(pl.multiple_of(block * wide, wide), wide)
        index = jnp.broadcast_to(order[0:1, rows].astype(F32), (128, wide)).T
        lane = lax.broadcasted_iota(jnp.int32, (wide, 128), 1).astype(F32)
        chosen = jnp.concatenate(
            [jnp.where(index == lane + 128.0 * j, 1.0, 0.0).astype(BF16) for j in range(leaf // 128)], 1)
        value = mm(chosen, charges[...])
        rhs[rows, :] = value.astype(BF16)
        rhst[:, rows] = value.T.astype(BF16)
        return carry

    lax.fori_loop(0, PARTS, permute, 0)

    loads[1].wait()
    own = mm(rhst[...], bases[...]).astype(BF16)
    c0[...] = own
    ut[...] = mm(own, lift[...].astype(BF16)).astype(BF16)
    up_near = send(ut.at[at_slot(1), :], rs.at[0], flip(1))
    up_cross = send(ut.at[at_slot(3), :], rs.at[1], flip(1))

    @pl.when(gives)
    def _():
        give_rhs[0].start()
        mate_rhs.start()

    mate_far = [send(c0, c0x.at[0], flip(1)), send(z0, z0x.at[0], flip(1))]
    for copy in phase_a2:
        copy.wait_recv()
    phase_a.append(send(z1.at[at_slot(2), :], z1.at[at_slot(2), :], flip(1)))
    phase_a.append(send(nl.at[at_slot(2), :], nl.at[at_slot(2), :], flip(1)))
    phase_a.append(send(z2.at[far16, :], z2.at[far16, :], flip(1)))
    loads[2].wait()

    def augment(block, carry):
        rows = pl.ds(pl.multiple_of(block * ROWS, ROWS), ROWS)
        p = points[rows, :]
        laug[rows, 0:dim] = (p.astype(F32) * (4.0 / dim)).astype(BF16)
        laug[rows, dim:] = norm_lanes(p, -2.0 / dim, -2.0 / dim, False)
        raug[rows, 0:dim] = p
        raug[rows, dim:] = norm_lanes(p, 1.0, 1.0, True)
        return carry

    first = near[0, 0] - me
    second = near[0, 1] - me
    one = 1 - 2 * (me % 2)
    near_one = jnp.logical_or(first == one, second == one)

    def choose(a, b):
        return jnp.where(near_one, a.astype(F32), b.astype(F32)).astype(BF16)

    def tiles(rows):
        left = laug[rows, :]
        return jnp.concatenate(
            [jnp.exp(mm(left, raug[j:j + 512, :], 1, 1)).astype(BF16) for j in range(0, leaf, 512)], 1)

    def own_tile(block):
        def body(b, carry):
            rows = pl.ds(pl.multiple_of(b * ROWS, ROWS), ROWS)
            acc[rows, :] = mm(tiles(rows), rhs[...])
            return carry

        lax.fori_loop(block, block + 1, body, 0)

    def carry_up():
        up_cross.wait_recv()
        us[...] = (ut[at_slot(2), :].astype(F32) + rs[1].astype(F32)).astype(BF16)
        up_two.start()

    def spread_proxies():
        for copy in phase_a:
            copy.wait_recv()
        for copy in phase_b:
            copy.start()

    def node_level():
        up_near.wait_recv()
        up_two.wait_recv()
        total = ut[mine, :].astype(F32) + rs[0].astype(F32) + rs[2].astype(F32)
        nv[0] = total.astype(BF16)
        nv[1] = mm(total.astype(BF16), nl[...]).astype(BF16)
        for copy in phase_two:
            copy.start()

    def top_level():
        for copy in phase_b + phase_two:
            copy.wait_recv()
        lifted = nv[1].astype(F32)
        for i in range(3):
            lifted = lifted + nvs[i, 1].astype(F32)
        c2[...] = lifted.astype(BF16)
        for copy in phase_top:
            copy.start()

    def fields_down():
        side = mm(nvs[0, 0], couple(z1s[0], z1[...]))
        for i in (1, 2):
            side = side + mm(nvs[i, 0], couple(z1s[i], z1[...]))
        for copy in phase_top:
            copy.wait_recv()
        field = mm(c2o[0], couple(z2o[0], z2[...]))
        for d in range(1, nodes - 1):
            field = field + mm(c2o[d], couple(z2o[d], z2[...]))
        field1 = side + mm(field.astype(BF16), nl[...], 1, 1)
        f1[mine, :] = field1.astype(BF16)
        down_two.start()
        down_one.start()

    def gather_down():
        down_two.wait_recv()
        down_rest.start()

    def descend(far):
        down_one.wait_recv()
        down_rest.wait_recv()
        f0[...] = (far() + mm(f1[...], lift[...].astype(BF16), 1, 1)).astype(BF16)

        def body(block, carry):
            rows = pl.ds(pl.multiple_of(block * ROWS, ROWS), ROWS)
            acc[rows, :] += mm(bases[rows, :], f0[...], 1, 1)
            return carry

        lax.fori_loop(0, blocks, body, 0)

    carry_up()
    lax.fori_loop(0, blocks, augment, 0)

    @pl.when(gives)
    def _():
        give_rhs[1].start()
        give_rhs[2].start()
        own_tile(0)
        spread_proxies()
        give_rhs[3].start()
        own_tile(1)
        node_level()
        give_rhs[4].start()
        mate_points.wait_recv()
        mate_rhs.wait_recv()

        def mate(block, carry):
            rows = pl.ds(pl.multiple_of(block * ROWS, ROWS), ROWS)
            p = p1[rows, :]
            raug[rows, 0:dim] = p
            raug[rows, dim:] = norm_lanes(p, 1.0, 1.0, True)
            rmask[rows, :] = jnp.where(near_one, r1[rows, :].astype(F32), 0.0).astype(BF16)
            return carry

        lax.fori_loop(0, blocks, mate, 0)

        def mate_tile(block):
            def body(b, carry):
                rows = pl.ds(pl.multiple_of(b * ROWS, ROWS), ROWS)
                acc[rows, :] += mm(tiles(rows), rmask[...])
                return carry

            lax.fori_loop(block, block + 1, body, 0)

        mate_tile(0)
        give_rhs[5].start()
        give_coeff.start()
        mate_tile(1)
        top_level()
        fields_down()
        give_rhs[6].start()
        give_rhs[7].start()
        gather_down()
        for copy in mate_far:
            copy.wait_recv()
        back_far.wait_recv()
        descend(lambda: jnp.where(
            near_one, frecv[...].astype(F32), mm(c0x[0], couple(z0x[0], z0[...]))))
        for k, copy in enumerate(back_part):
            copy.wait_recv()
            out[part_rows[k], :] = (acc[part_rows[k], :] + xrecv[k].astype(F32)).astype(BF16)
        for copy in (give_points + give_detour + [give_proxy, give_coeff] + give_rhs):
            copy.wait_send()

    @pl.when(works)
    def _():
        def take_points(k):
            (give_points[k] if k < half else detour_on[k - half]).wait_recv()
            share_points[k].start()

        def pass_on(k):
            give_detour[k].wait_recv()
            detour_on[k].start()

        def part(tile, k, picked):
            saug[:, 0:dim] = picked
            saug[:, dim:] = norm_lanes(picked, 1.0, 1.0, True)

            def body(block, carry):
                rows = pl.ds(pl.multiple_of(block * ROWS, ROWS), ROWS)
                tile[k, rows, :] = jnp.exp(mm(laug[rows, :], saug[...], 1, 1)).astype(BF16)
                return carry

            lax.fori_loop(0, blocks, body, 0)
            return mm(rhst[...], tile[k]).T

        def diagonal(k):
            share_points[k].wait_recv()
            dsend[k] = part(t2, k, p3[part_rows[k], :]).astype(BF16)
            cross_part[k].start()

        def chosen(k):
            value = part(t1, k, choose(p1[part_rows[k], :], p2[part_rows[k], :]))
            racc[...] = jnp.where(near_one, 0.0, value)

        def combine(k):
            cross_part[k].wait_recv()
            xsend[k] = (racc[...] + drecv[k].astype(F32)).astype(BF16)

        take_points(0)
        pass_on(0)
        diagonal(0)
        pass_on(1)
        mate_points.wait_recv()
        chosen(0)
        take_points(1)
        combine(0)
        back_part[0].start()
        diagonal(1)
        spread_proxies()
        chosen(1)
        take_points(2)
        combine(1)
        back_part[1].start()
        mate_rhs.start()
        diagonal(2)
        chosen(2)
        take_points(3)
        combine(2)
        back_part[2].start()
        node_level()
        diagonal(3)
        chosen(3)
        combine(3)
        give_proxy.wait_recv()
        fsend[...] = jnp.where(near_one, mm(c0[...], couple(z0[...], z0x[1])), 0.0).astype(BF16)
        top_level()
        own_tile(0)
        fields_down()
        back_far.start()
        back_part[3].start()

        def take_rhs(j):
            give_rhs[j].wait_recv()
            share_rhs[j].start()

        def apply(j, final):
            k, at = divmod(j * step, wide)
            cr[...] = choose(r1[step_rows[j], :], r2[step_rows[j], :])

            def body(block, carry):
                rows = pl.ds(pl.multiple_of(block * ROWS, ROWS), ROWS)
                value = acc[rows, :] + mm(t1[k, rows, at:at + step], cr[...])
                value = value + mm(t2[k, rows, at:at + step], r3[step_rows[j], :])
                if final:
                    out[rows, :] = value.astype(BF16)
                else:
                    acc[rows, :] = value
                return carry

            lax.fori_loop(0, blocks, body, 0)

        take_rhs(0)
        take_rhs(1)
        take_rhs(2)
        own_tile(1)
        mate_rhs.wait_recv()
        for j in range(CHUNKS):
            if j + 3 < CHUNKS:
                take_rhs(j + 3)
            share_rhs[j].wait_recv()
            if j == CHUNKS - 1:
                gather_down()
                for copy in mate_far:
                    copy.wait_recv()
                give_coeff.wait_recv()
                descend(lambda: mm(choose(c0x[1], c0x[0]), couple(choose(z0x[1], z0x[0]), z0[...])))
            apply(j, j == CHUNKS - 1)
        for copy in (detour_on + share_points + share_rhs + cross_part + back_part + [back_far]):
            copy.wait_send()

    for copy in started + [mate_rhs, up_two, down_two, down_one, down_rest] + phase_b + phase_two + phase_top:
        copy.wait_send()


def per_device(n, near, points, charges, order, bases, lift, nlift, zleaf, znode, ztop):
    leaf, dim = points.shape
    nrhs = charges.shape[1]
    rank = lift.shape[0]
    quarter = rank // 4
    nodes = n // 16
    wide, step = leaf // PARTS, leaf // CHUNKS
    copies = 60 + 3 * PARTS + 2 * CHUNKS + 2 * nodes
    v = pltpu.VMEM
    vmem = pl.BlockSpec(memory_space=pltpu.VMEM)
    return pl.pallas_call(
        functools.partial(kernel, n),
        out_shape=jax.ShapeDtypeStruct((leaf, nrhs), BF16),
        in_specs=[pl.BlockSpec(memory_space=pltpu.SMEM)] + [pl.BlockSpec(memory_space=pl.ANY)] * 3 + [vmem] * 6,
        out_specs=vmem,
        scratch_shapes=[
            v((leaf, dim), BF16), v((leaf, nrhs), BF16), v((leaf, rank), BF16),
            v((leaf, nrhs), BF16), v((nrhs, leaf), BF16), v((leaf, 2 * dim), BF16), v((leaf, 2 * dim), BF16),
            v((leaf, nrhs), F32),
            v((leaf, dim), BF16), v((leaf, dim), BF16), v((leaf, dim), BF16),
            v((leaf, nrhs), BF16), v((leaf, nrhs), BF16), v((leaf, nrhs), BF16), v((leaf, nrhs), BF16),
            v((leaf // 2, dim), BF16),
            v((PARTS, leaf, wide), BF16), v((PARTS, leaf, wide), BF16),
            v((wide, 2 * dim), BF16), v((step, nrhs), BF16), v((wide, nrhs), F32),
            v((PARTS, wide, nrhs), BF16), v((PARTS, wide, nrhs), BF16),
            v((PARTS, wide, nrhs), BF16), v((PARTS, wide, nrhs), BF16),
            v((nrhs, rank), BF16), v((nrhs, rank), BF16),
            v((nrhs, rank), BF16), v((2, nrhs, rank), BF16),
            v((rank, dim), BF16), v((2, rank, dim), BF16),
            v((nrhs, rank), BF16), v((quarter, rank), BF16), v((3, quarter, rank), BF16),
            v((rank, rank), BF16), v((rank, dim), BF16), v((3, rank, dim), BF16),
            v((rank, dim), BF16),
            v((2, quarter, rank), BF16), v((3, 2, quarter, rank), BF16),
            v((quarter, rank), BF16), v((nodes - 1, quarter, rank), BF16),
            v((nodes - 1, rank, dim), BF16), v((nrhs, rank), BF16), v((nrhs, rank), BF16),
            pltpu.SemaphoreType.DMA((copies,)), pltpu.SemaphoreType.DMA((copies,)),
            pltpu.SemaphoreType.DMA((3,)),
        ],
        compiler_params=pltpu.CompilerParams(
            collective_id=0, has_side_effects=True, vmem_limit_bytes=VMEM_MB * 1024 * 1024),
    )(near, points, charges, bases, order, lift, nlift, zleaf, znode, ztop)


def solution(mesh):
    n = mesh.shape["leaf"]

    def body(points, charges, order, near, bases, lift, nlift, zleaf, znode, ztop):
        return per_device(n, near, points, charges, order, bases, lift, nlift, zleaf, znode, ztop)

    return jax.shard_map(
        body, mesh=mesh, in_specs=(P("leaf", None),) * 10, out_specs=P("leaf", None), check_vma=False)
```

```python
import functools

import jax
import jax.numpy as jnp
from jax import lax
from jax.experimental import pallas as pl
from jax.experimental.pallas import tpu as pltpu
from jax.sharding import PartitionSpec as P

MESH = pl.DeviceIdType.MESH
F32, BF16 = jnp.float32, jnp.bfloat16
CHUNKS = 8
PARTS = 4
ROWS = 1024
VMEM_MB = 50


def mm(a, b, ca=1, cb=0):
    return lax.dot_general(a, b, (((ca,), (cb,)), ((), ())), preferred_element_type=F32)


def split3(x):
    high = x.astype(BF16).astype(F32)
    middle = (x - high).astype(BF16).astype(F32)
    return high, middle, x - high - middle


def norm_column(p):
    wide = p.astype(F32)
    return jnp.sum(wide * wide, axis=1, keepdims=True)


def norm_lanes(p, one_scale, norm_scale, norm_first):
    high, middle, low = split3(norm_column(p))
    lane = lax.broadcasted_iota(jnp.int32, (p.shape[0], 128), 1)
    first = 0 if norm_first else 3
    ones = jnp.where(lane < 6, one_scale, 0.0)
    out = jnp.where(lane == first, high * norm_scale, ones)
    out = jnp.where(lane == first + 1, middle * norm_scale, out)
    out = jnp.where(lane == first + 2, low * norm_scale, out)
    return out.astype(BF16)


def couple(left, right):
    scale = 2.0 / left.shape[1]
    wide = right.astype(F32)
    square = wide * wide
    high = square.astype(BF16)
    low = (square - high.astype(F32)).astype(BF16)
    ones = jnp.ones((8, left.shape[1]), BF16)
    right_norm = (mm(ones, high, 1, 1) + mm(ones, low, 1, 1))[0:1, :]
    return jnp.exp((2.0 * mm(left, right, 1, 1) - norm_column(left) - right_norm) * scale).astype(BF16)


def kernel(n, near_in, points_in, charges_in, bases_in, order_in, lift_in, nlift_in, zleaf_in, znode_in, ztop_in, out,
           near, points, charges, bases, order, lift, nlift, zleaf, znode, ztop, rhs, laug, raug, acc, acct,
           p1, p2, p3, r1, r2, r3, rmask, prel,
           t1, t2, saug, racc, dsend, drecv, xsend, xrecv, fsend, frecv,
           c0, c0x, z0, z0x, ut, us, rs, nl, z1, z1s, z2, nv, nvs, c2, c2o, z2o, f1, f0,
           ssem, rsem, lsem):
    me = lax.axis_index("leaf")
    leaf, dim = points.shape
    rank = lift.shape[0]
    quarter = rank // 4
    sixteenth = rank // 16
    nodes = n // 16
    slot = me % 4
    group = me // 4 % 4
    part = me % 16
    node = me // 16
    step = leaf // CHUNKS
    wide = leaf // PARTS
    half = PARTS // 2
    blocks = leaf // ROWS
    gives = (me // 2 + me // 4) % 2 == 0
    works = (me // 2 + me // 4) % 2 == 1

    def flip(bits):
        where = me
        for bit in (1, 2, 4, 8):
            if bits & bit:
                where = where + bit - 2 * bit * (me // bit % 2)
        return where

    def flip_slot(bits):
        return flip(bits) % 4

    others = [(node + d) % nodes * 16 + part for d in range(1, nodes)]

    barrier = pltpu.get_barrier_semaphore()
    partners = [flip(b) for b in (1, 2, 4, 6, 8, 12)] + others
    for other in partners:
        pl.semaphore_signal(barrier, inc=1, device_id=(other,), device_id_type=MESH)

    loads = [pltpu.make_async_copy(a, b, lsem.at[i]) for i, (a, b) in enumerate((
        (znode_in, znode), (nlift_in, nlift), (ztop_in, ztop), (zleaf_in, zleaf), (order_in, order), (charges_in, charges),
        (bases_in, bases), (lift_in, lift), (points_in, points), (near_in, near)))]
    for copy in loads:
        copy.start()
    def start(copies):
        for copy in copies:
            copy.start()

    def arrive(copies):
        for copy in copies:
            copy.wait_recv()

    count = [0]

    def link(src, dst, device):
        i = count[0]
        count[0] += 1
        return pltpu.make_async_remote_copy(
            src_ref=src, dst_ref=dst, send_sem=ssem.at[i], recv_sem=rsem.at[i],
            device_id=(device,), device_id_type=MESH)

    def at_slot(bits):
        where = flip_slot(bits) if bits else slot
        return pl.ds(pl.multiple_of(where * quarter, quarter), quarter)

    mine = at_slot(0)
    mine16 = pl.ds(pl.multiple_of(part * sixteenth, sixteenth), sixteenth)
    far16 = pl.ds(pl.multiple_of(flip(2) % 16 * sixteenth, sixteenth), sixteenth)
    mine64 = pl.ds(pl.multiple_of(group * quarter, quarter), quarter)
    part_rows = [pl.ds(k * wide, wide) for k in range(PARTS)]
    step_rows = [pl.ds(j * step, step) for j in range(CHUNKS)]

    give_points = [link(points_in.at[r, :], p2.at[r, :], flip(2)) for r in part_rows[:half]]
    give_detour = [link(points_in.at[r, :], prel.at[pl.ds(k * wide, wide), :], flip(4))
                   for k, r in enumerate(part_rows[half:])]
    detour_on = [link(prel.at[pl.ds(k * wide, wide), :], p2.at[r, :], flip(6))
                 for k, r in enumerate(part_rows[half:])]
    give_proxy = link(z0, z0x.at[1], flip(2))
    give_coeff = link(c0, c0x.at[1], flip(2))
    give_rhs = [link(rhs.at[r, :], r2.at[r, :], flip(2)) for r in step_rows]
    share_points = [link(p2.at[r, :], p3.at[r, :], flip(1)) for r in part_rows]
    share_rhs = [link(r2.at[r, :], r3.at[r, :], flip(1)) for r in step_rows]
    cross_part = [link(dsend.at[k], drecv.at[k], flip(1)) for k in range(PARTS)]
    back_part = [link(xsend.at[k], xrecv.at[k], flip(2)) for k in range(PARTS)]
    back_far = link(fsend, frecv, flip(2))
    proxies_two = [link(z1.at[mine, :], z1.at[mine, :], flip(2)),
                   link(nl.at[mine, :], nl.at[mine, :], flip(2)),
                   link(z2.at[mine16, :], z2.at[mine16, :], flip(2))]
    proxies_one = [link(z1.at[mine, :], z1.at[mine, :], flip(1)),
                   link(nl.at[mine, :], nl.at[mine, :], flip(1)),
                   link(z2.at[mine16, :], z2.at[mine16, :], flip(1))]
    proxies_rest = [link(z1.at[at_slot(2), :], z1.at[at_slot(2), :], flip(1)),
                    link(nl.at[at_slot(2), :], nl.at[at_slot(2), :], flip(1)),
                    link(z2.at[far16, :], z2.at[far16, :], flip(1))]
    mate_points = link(points_in, p1, flip(1))
    mate_far = [link(c0, c0x.at[0], flip(1)), link(z0, z0x.at[0], flip(1))]
    up_near = link(ut.at[at_slot(1), :], rs.at[0], flip(1))
    up_cross = link(ut.at[at_slot(3), :], rs.at[1], flip(1))
    mate_rhs = link(rhs, r1, flip(1))
    up_two = link(us, rs.at[2], flip(2))
    phase_b = []
    for i, b in enumerate((4, 8, 12)):
        phase_b.append(link(z1, z1s.at[i], flip(b)))
        phase_b.append(link(z2.at[mine64, :], z2.at[mine64, :], flip(b)))
    phase_two = [link(nv, nvs.at[i], flip(b)) for i, b in enumerate((4, 8, 12))]
    top_proxies = [link(z2, z2o.at[d], other) for d, other in enumerate(others)]
    top_coeffs = [link(c2, c2o.at[d], other) for d, other in enumerate(others)]
    down_two = link(f1.at[mine, :], f1.at[mine, :], flip(2))
    down_one = link(f1.at[mine, :], f1.at[mine, :], flip(1))
    down_rest = link(f1.at[at_slot(2), :], f1.at[at_slot(2), :], flip(1))

    for copy in loads[:4]:
        copy.wait()
    z1[mine, :] = znode[...].astype(BF16)
    nl[mine, :] = nlift[...].astype(BF16)
    z2[mine16, :] = ztop[...].astype(BF16)
    z0[...] = zleaf[...].astype(BF16)

    def enter(copies):
        pl.semaphore_wait(barrier, len(partners))
        start(copies)

    @pl.when(gives)
    def _():
        enter(give_points[:1] + proxies_two + give_points[1:] + give_detour + [give_proxy] + proxies_one + [mate_points])

    loads[4].wait()
    loads[5].wait()

    def permute(block, carry):
        rows = pl.ds(pl.multiple_of(block * wide, wide), wide)
        index = jnp.broadcast_to(order[0:1, rows].astype(F32), (128, wide)).T
        lane = lax.broadcasted_iota(jnp.int32, (wide, 128), 1).astype(F32)
        chosen = jnp.concatenate(
            [jnp.where(index == lane + 128.0 * j, 1.0, 0.0).astype(BF16) for j in range(leaf // 128)], 1)
        value = mm(chosen, charges[...])
        rhs[rows, :] = value.astype(BF16)
        return carry

    lax.fori_loop(0, PARTS, permute, 0)

    @pl.when(works)
    def _():
        enter(proxies_two + proxies_one + [mate_points])

    loads[6].wait()
    loads[7].wait()
    own = mm(rhs[...], bases[...], 0, 0).astype(BF16)
    c0[...] = own
    ut[...] = mm(own, lift[...].astype(BF16)).astype(BF16)
    start([up_near, up_cross] + mate_far)
    loads[8].wait()
    loads[9].wait()

    def augment(block, carry):
        rows = pl.ds(pl.multiple_of(block * ROWS, ROWS), ROWS)
        p = points[rows, :]
        laug[rows, 0:dim] = (p.astype(F32) * (4.0 / dim)).astype(BF16)
        laug[rows, dim:] = norm_lanes(p, -2.0 / dim, -2.0 / dim, False)
        raug[rows, 0:dim] = p
        raug[rows, dim:] = norm_lanes(p, 1.0, 1.0, True)
        return carry

    first = near[0, 0] - me
    second = near[0, 1] - me
    one = 1 - 2 * (me % 2)
    near_one = jnp.logical_or(first == one, second == one)

    def choose(a, b):
        return jnp.where(near_one, a.astype(F32), b.astype(F32)).astype(BF16)

    def tiles(rows):
        left = laug[rows, :]
        return jnp.concatenate(
            [jnp.exp(mm(left, raug[j:j + 512, :], 1, 1)).astype(BF16) for j in range(0, leaf, 512)], 1)

    def own_tile(first, last):
        def body(b, carry):
            rows = pl.ds(pl.multiple_of(b * ROWS, ROWS), ROWS)
            acc[rows, :] = mm(tiles(rows), rhs[...])
            return carry

        lax.fori_loop(first, last, body, 0)

    def carry_up():
        us[...] = (ut[at_slot(2), :].astype(F32) + rs[1].astype(F32)).astype(BF16)

    def node_level():
        total = ut[mine, :].astype(F32) + rs[0].astype(F32) + rs[2].astype(F32)
        nv[0] = total.astype(BF16)
        nv[1] = mm(total.astype(BF16), nl[...]).astype(BF16)

    def top_level():
        lifted = nv[1].astype(F32)
        for i in range(3):
            lifted = lifted + nvs[i, 1].astype(F32)
        c2[...] = lifted.astype(BF16)

    def fields_down():
        side = mm(nvs[0, 0], couple(z1s[0], z1[...]))
        for i in (1, 2):
            side = side + mm(nvs[i, 0], couple(z1s[i], z1[...]))
        field = mm(c2o[0], couple(z2o[0], z2[...]))
        for d in range(1, nodes - 1):
            field = field + mm(c2o[d], couple(z2o[d], z2[...]))
        field1 = side + mm(field.astype(BF16), nl[...], 1, 1)
        f1[mine, :] = field1.astype(BF16)

    def descend(far):
        f0[...] = (far() + mm(f1[...], lift[...].astype(BF16), 1, 1)).astype(BF16)

        def body(block, carry):
            rows = pl.ds(pl.multiple_of(block * ROWS, ROWS), ROWS)
            acc[rows, :] += mm(bases[rows, :], f0[...], 1, 1)
            return carry

        lax.fori_loop(0, blocks, body, 0)

    lax.fori_loop(0, blocks, augment, 0)

    @pl.when(gives)
    def _():
        arrive([up_cross])
        carry_up()
        start([up_two, give_rhs[0], mate_rhs])
        arrive(proxies_two)
        start(proxies_rest + [give_rhs[1]])
        own_tile(0, blocks // 2)
        arrive(proxies_one + proxies_rest + [up_near, up_two])
        start(phase_b)
        node_level()
        start(phase_two + give_rhs[2:4])
        own_tile(blocks // 2, blocks)
        arrive(phase_b + [mate_points, mate_rhs])
        start(top_proxies + [give_rhs[4]])

        def mate(block, carry):
            rows = pl.ds(pl.multiple_of(block * ROWS, ROWS), ROWS)
            p = p1[rows, :]
            raug[rows, 0:dim] = p
            raug[rows, dim:] = norm_lanes(p, 1.0, 1.0, True)
            rmask[rows, :] = jnp.where(near_one, r1[rows, :].astype(F32), 0.0).astype(BF16)
            return carry

        lax.fori_loop(0, blocks, mate, 0)

        def mate_tile(b, carry):
            rows = pl.ds(pl.multiple_of(b * ROWS, ROWS), ROWS)
            acc[rows, :] += mm(tiles(rows), rmask[...])
            return carry

        lax.fori_loop(0, blocks, mate_tile, 0)
        start([give_rhs[5], give_coeff])
        arrive(phase_two)
        top_level()
        start(top_coeffs)
        arrive(top_proxies + top_coeffs)
        fields_down()
        start([down_two, down_one] + give_rhs[6:])
        arrive([down_two])
        start([down_rest])
        arrive([down_one, down_rest, back_far] + mate_far)
        descend(lambda: jnp.where(
            near_one, frecv[...].astype(F32), mm(c0x[0], couple(z0x[0], z0[...]))))
        for k, copy in enumerate(back_part):
            copy.wait_recv()
            out[part_rows[k], :] = (acc[part_rows[k], :] + xrecv[k].astype(F32)).astype(BF16)
        for copy in give_points + give_detour + [give_proxy, give_coeff] + give_rhs:
            copy.wait_send()

    @pl.when(works)
    def _():
        def part(tile, k, picked):
            saug[k % 2, :, 0:dim] = picked
            saug[k % 2, :, dim:] = norm_lanes(picked, 1.0, 1.0, True)
            values = jnp.concatenate(
                [jnp.exp(mm(saug[k % 2], laug[j:j + 512, :], 1, 1)).astype(BF16) for j in range(0, leaf, 512)], 1)
            tile[part_rows[k], :] = values
            return mm(values, rhs[...])

        def diagonal(k):
            dsend[k] = part(t2, k, p3[part_rows[k], :]).astype(BF16)

        def chosen(k):
            value = part(t1, k, choose(p1[part_rows[k], :], p2[part_rows[k], :]))
            racc[k % 2] = jnp.where(near_one, 0.0, value)

        def combine(k):
            xsend[k] = (racc[k % 2] + drecv[k].astype(F32)).astype(BF16)

        arrive([give_points[0], mate_points, up_cross])
        start([share_points[0]])
        carry_up()
        start([up_two])
        arrive([give_detour[0]])
        start([detour_on[0]])
        chosen(0)
        arrive([share_points[0]] + proxies_two)
        start(proxies_rest)
        diagonal(0)
        start([cross_part[0]])
        arrive([give_points[1], give_detour[1]])
        start([share_points[1], detour_on[1]])
        chosen(1)
        arrive([cross_part[0]])
        combine(0)
        start([back_part[0]])
        arrive([share_points[1]] + proxies_one + proxies_rest)
        start(phase_b)
        diagonal(1)
        start([cross_part[1]])
        arrive([detour_on[0]])
        start([share_points[2]])
        chosen(2)
        arrive([cross_part[1], share_points[2], detour_on[1], up_near, up_two])
        start([share_points[3]])
        node_level()
        start(phase_two)
        combine(1)
        diagonal(2)
        start([back_part[1], cross_part[2]])
        arrive([share_points[3]] + phase_b)
        start(top_proxies)
        chosen(3)
        arrive([cross_part[2]])
        combine(2)
        diagonal(3)
        start([back_part[2], cross_part[3], mate_rhs])
        arrive(phase_two + [give_proxy])
        top_level()
        fsend[...] = jnp.where(near_one, mm(c0[...], couple(z0[...], z0x[1])), 0.0).astype(BF16)
        start(top_coeffs + [back_far])
        arrive(give_rhs[:3] + [cross_part[3]])
        start(share_rhs[:3])
        combine(3)
        own_tile(0, blocks)
        arrive(top_proxies + top_coeffs + give_rhs[3:5])
        start(share_rhs[3:5])
        fields_down()
        start([down_two, down_one, back_part[3]])

        def pick_rhs(rows):
            return choose(r1[rows, :], r2[rows, :]), r3[rows, :]

        def apply(first, last):
            rows = pl.ds(first * step, (last - first) * step)
            near_rhs, far_rhs = pick_rhs(rows)
            value = mm(near_rhs, t1[rows, :], 0, 0) + mm(far_rhs, t2[rows, :], 0, 0)
            acct[...] = value if first == 0 else acct[...] + value

        def finish(j):
            near_rhs, far_rhs = pick_rhs(step_rows[j])
            return mm(t1[step_rows[j], :], near_rhs, 0, 0) + mm(t2[step_rows[j], :], far_rhs, 0, 0)

        arrive(share_rhs[:4] + [mate_rhs])
        apply(0, 4)
        arrive([give_rhs[5], down_two])
        start([share_rhs[5], down_rest])
        arrive([down_one, give_coeff, share_rhs[4], share_rhs[5]] + mate_far)
        apply(4, 6)
        arrive([down_rest])
        descend(lambda: mm(choose(c0x[1], c0x[0]), couple(choose(z0x[1], z0x[0]), z0[...])))
        for j in range(PARTS):
            acc[part_rows[j], :] += acct[:, j * wide:(j + 1) * wide].T
        arrive([give_rhs[6]])
        start([share_rhs[6]])
        arrive([share_rhs[6]])
        acc[...] += finish(6)
        arrive([give_rhs[7]])
        start([share_rhs[7]])
        arrive([share_rhs[7]])
        out[...] = (acc[...] + finish(7)).astype(BF16)
        for copy in detour_on + share_points + share_rhs + cross_part + back_part + [back_far]:
            copy.wait_send()

    for copy in (proxies_two + proxies_one + proxies_rest + mate_far + phase_b + phase_two + top_proxies + top_coeffs
                 + [mate_points, mate_rhs, up_near, up_cross, up_two, down_two, down_one, down_rest]):
        copy.wait_send()


def per_device(n, near, points, charges, order, bases, lift, nlift, zleaf, znode, ztop):
    leaf, dim = points.shape
    nrhs = charges.shape[1]
    rank = lift.shape[0]
    quarter = rank // 4
    nodes = n // 16
    wide, step = leaf // PARTS, leaf // CHUNKS
    copies = 60 + 3 * PARTS + 2 * CHUNKS + 2 * nodes
    v = pltpu.VMEM
    vmem = pl.BlockSpec(memory_space=pltpu.VMEM)
    return pl.pallas_call(
        functools.partial(kernel, n),
        out_shape=jax.ShapeDtypeStruct((leaf, nrhs), BF16),
        in_specs=[pl.BlockSpec(memory_space=pltpu.HBM)] * 10,
        out_specs=vmem,
        scratch_shapes=[
            pltpu.SMEM(near.shape, near.dtype),
            v((leaf, dim), BF16), v((leaf, nrhs), BF16), v((leaf, rank), BF16), v(order.shape, order.dtype),
            v(lift.shape, F32), v(nlift.shape, F32), v(zleaf.shape, F32), v(znode.shape, F32), v(ztop.shape, F32),
            v((leaf, nrhs), BF16), v((leaf, 2 * dim), BF16), v((leaf, 2 * dim), BF16),
            v((leaf, nrhs), F32), v((nrhs, leaf), F32),
            v((leaf, dim), BF16), v((leaf, dim), BF16), v((leaf, dim), BF16),
            v((leaf, nrhs), BF16), v((leaf, nrhs), BF16), v((leaf, nrhs), BF16), v((leaf, nrhs), BF16),
            v((leaf // 2, dim), BF16),
            v((leaf, leaf), BF16), v((leaf, leaf), BF16),
            v((2, wide, 2 * dim), BF16), v((2, wide, nrhs), F32),
            v((PARTS, wide, nrhs), BF16), v((PARTS, wide, nrhs), BF16),
            v((PARTS, wide, nrhs), BF16), v((PARTS, wide, nrhs), BF16),
            v((nrhs, rank), BF16), v((nrhs, rank), BF16),
            v((nrhs, rank), BF16), v((2, nrhs, rank), BF16),
            v((rank, dim), BF16), v((2, rank, dim), BF16),
            v((nrhs, rank), BF16), v((quarter, rank), BF16), v((3, quarter, rank), BF16),
            v((rank, rank), BF16), v((rank, dim), BF16), v((3, rank, dim), BF16),
            v((rank, dim), BF16),
            v((2, quarter, rank), BF16), v((3, 2, quarter, rank), BF16),
            v((quarter, rank), BF16), v((nodes - 1, quarter, rank), BF16),
            v((nodes - 1, rank, dim), BF16), v((nrhs, rank), BF16), v((nrhs, rank), BF16),
            pltpu.SemaphoreType.DMA((copies,)), pltpu.SemaphoreType.DMA((copies,)),
            pltpu.SemaphoreType.DMA((10,)),
        ],
        compiler_params=pltpu.CompilerParams(
            collective_id=0, has_side_effects=True, vmem_limit_bytes=VMEM_MB * 1024 * 1024),
    )(*(pltpu.with_memory_space_constraint(x, pltpu.HBM) for x in (
        near, points, charges, bases, order, lift, nlift, zleaf, znode, ztop)))


def solution(mesh):
    n = mesh.shape["leaf"]

    def body(points, charges, order, near, bases, lift, nlift, zleaf, znode, ztop):
        return per_device(n, near, points, charges, order, bases, lift, nlift, zleaf, znode, ztop)

    return jax.shard_map(
        body, mesh=mesh, in_specs=(P("leaf", None),) * 10, out_specs=P("leaf", None), check_vma=False)
```

```python
import functools

import jax
import jax.numpy as jnp
from jax import lax
from jax.experimental import pallas as pl
from jax.experimental.pallas import tpu as pltpu
from jax.sharding import PartitionSpec as P

MESH = pl.DeviceIdType.MESH
F32, BF16 = jnp.float32, jnp.bfloat16
CHUNKS = 8
PARTS = 4
ROWS = 1024
VMEM_MB = 50


def mm(a, b, ca=1, cb=0):
    return lax.dot_general(a, b, (((ca,), (cb,)), ((), ())), preferred_element_type=F32)


def split3(x):
    high = x.astype(BF16).astype(F32)
    middle = (x - high).astype(BF16).astype(F32)
    return high, middle, x - high - middle


def norm_column(p):
    wide = p.astype(F32)
    return jnp.sum(wide * wide, axis=1, keepdims=True)


def norm_lanes(p, one_scale, norm_scale, norm_first):
    high, middle, low = split3(norm_column(p))
    lane = lax.broadcasted_iota(jnp.int32, (p.shape[0], 128), 1)
    first = 0 if norm_first else 3
    ones = jnp.where(lane < 6, one_scale, 0.0)
    out = jnp.where(lane == first, high * norm_scale, ones)
    out = jnp.where(lane == first + 1, middle * norm_scale, out)
    out = jnp.where(lane == first + 2, low * norm_scale, out)
    return out.astype(BF16)


def couple(left, right):
    scale = 2.0 / left.shape[1]
    wide = right.astype(F32)
    square = wide * wide
    high = square.astype(BF16)
    low = (square - high.astype(F32)).astype(BF16)
    ones = jnp.ones((8, left.shape[1]), BF16)
    right_norm = (mm(ones, high, 1, 1) + mm(ones, low, 1, 1))[0:1, :]
    return jnp.exp((2.0 * mm(left, right, 1, 1) - norm_column(left) - right_norm) * scale).astype(BF16)


def kernel(n, near_in, points_in, charges_in, bases_in, order_in, lift_in, nlift_in, zleaf_in, znode_in, ztop_in, out,
           near, points, charges, bases, order, lift, nlift, zleaf, znode, ztop, rhs, laug, raug, acc, acct,
           p1, p2, p3, r1, r2, r3, rmask, prel, zrel,
           t1, t2, saug, racc, dsend, drecv, xsend, xrecv, fsend, frecv,
           c0, c0x, z0, z0x, ut, us, rs, nl, z1, z1s, z2, nv, nvs, c2, c2o, z2o, f1, f0,
           ssem, rsem, lsem):
    me = lax.axis_index("leaf")
    leaf, dim = points.shape
    rank = lift.shape[0]
    quarter = rank // 4
    sixteenth = rank // 16
    nodes = n // 16
    slot = me % 4
    group = me // 4 % 4
    part = me % 16
    node = me // 16
    step = leaf // CHUNKS
    wide = leaf // PARTS
    half = PARTS // 2
    blocks = leaf // ROWS
    gives = (me // 2 + me // 4 + me // 8) % 2 == 0
    works = (me // 2 + me // 4 + me // 8) % 2 == 1

    def flip(bits):
        where = me
        for bit in (1, 2, 4, 8):
            if bits & bit:
                where = where + bit - 2 * bit * (me // bit % 2)
        return where

    def flip_slot(bits):
        return flip(bits) % 4

    others = [(node + d) % nodes * 16 + part for d in range(1, nodes)]

    barrier = pltpu.get_barrier_semaphore()
    partners = [flip(b) for b in (1, 2, 4, 6, 8, 10, 12)] + others
    for other in partners:
        pl.semaphore_signal(barrier, inc=1, device_id=(other,), device_id_type=MESH)

    loads = [pltpu.make_async_copy(a, b, lsem.at[i]) for i, (a, b) in enumerate((
        (znode_in, znode), (nlift_in, nlift), (ztop_in, ztop), (zleaf_in, zleaf), (order_in, order), (charges_in, charges),
        (bases_in, bases), (lift_in, lift), (points_in, points), (near_in, near)))]
    for copy in loads:
        copy.start()
    def start(copies):
        for copy in copies:
            copy.start()

    def arrive(copies):
        for copy in copies:
            copy.wait_recv()

    count = [0]

    def link(src, dst, device):
        i = count[0]
        count[0] += 1
        return pltpu.make_async_remote_copy(
            src_ref=src, dst_ref=dst, send_sem=ssem.at[i], recv_sem=rsem.at[i],
            device_id=(device,), device_id_type=MESH)

    def at_slot(bits):
        where = flip_slot(bits) if bits else slot
        return pl.ds(pl.multiple_of(where * quarter, quarter), quarter)

    mine = at_slot(0)
    mine16 = pl.ds(pl.multiple_of(part * sixteenth, sixteenth), sixteenth)
    far16 = pl.ds(pl.multiple_of(flip(2) % 16 * sixteenth, sixteenth), sixteenth)
    mine64 = pl.ds(pl.multiple_of(group * quarter, quarter), quarter)
    part_rows = [pl.ds(k * wide, wide) for k in range(PARTS)]
    step_rows = [pl.ds(j * step, step) for j in range(CHUNKS)]

    give_points = [link(points_in.at[r, :], p2.at[r, :], flip(2)) for r in part_rows[:half]]
    detour_rows = [(pl.ds(half * wide + q * step, step), pl.ds(q * step, step)) for q in range(CHUNKS // 2)]
    give_detour = [link(points_in.at[r, :], prel.at[at, :], flip((4, 10)[q % 2]))
                   for q, (r, at) in enumerate(detour_rows)]
    detour_on = [link(prel.at[at, :], p2.at[r, :], flip((6, 8)[q % 2])) for q, (r, at) in enumerate(detour_rows)]
    give_proxy = link(z0, zrel, flip(10))
    proxy_on = link(zrel, z0x.at[1], flip(8))
    give_coeff = link(c0, c0x.at[1], flip(2))
    give_rhs = [link(rhs.at[r, :], r2.at[r, :], flip(2)) for r in step_rows]
    share_points = [link(p2.at[r, :], p3.at[r, :], flip(1)) for r in part_rows]
    share_rhs = [link(r2.at[r, :], r3.at[r, :], flip(1)) for r in step_rows]
    cross_part = [link(dsend.at[k], drecv.at[k], flip(1)) for k in range(PARTS)]
    back_part = [link(xsend.at[k], xrecv.at[k], flip(2)) for k in range(PARTS)]
    back_far = link(fsend, frecv, flip(2))
    proxies_two = [link(z1.at[mine, :], z1.at[mine, :], flip(2)),
                   link(nl.at[mine, :], nl.at[mine, :], flip(2)),
                   link(z2.at[mine16, :], z2.at[mine16, :], flip(2))]
    proxies_one = [link(z1.at[mine, :], z1.at[mine, :], flip(1)),
                   link(nl.at[mine, :], nl.at[mine, :], flip(1)),
                   link(z2.at[mine16, :], z2.at[mine16, :], flip(1))]
    proxies_rest = [link(z1.at[at_slot(2), :], z1.at[at_slot(2), :], flip(1)),
                    link(nl.at[at_slot(2), :], nl.at[at_slot(2), :], flip(1)),
                    link(z2.at[far16, :], z2.at[far16, :], flip(1))]
    mate_points = link(points_in, p1, flip(1))
    mate_far = [link(c0, c0x.at[0], flip(1)), link(z0, z0x.at[0], flip(1))]
    up_near = link(ut.at[at_slot(1), :], rs.at[0], flip(1))
    up_cross = link(ut.at[at_slot(3), :], rs.at[1], flip(1))
    mate_rhs = link(rhs, r1, flip(1))
    up_two = link(us, rs.at[2], flip(2))
    phase_b = []
    for i, b in enumerate((4, 8, 12)):
        phase_b.append(link(z1, z1s.at[i], flip(b)))
        phase_b.append(link(z2.at[mine64, :], z2.at[mine64, :], flip(b)))
    phase_two = [link(nv, nvs.at[i], flip(b)) for i, b in enumerate((4, 8, 12))]
    top_proxies = [link(z2, z2o.at[d], other) for d, other in enumerate(others)]
    top_coeffs = [link(c2, c2o.at[d], other) for d, other in enumerate(others)]
    down_two = link(f1.at[mine, :], f1.at[mine, :], flip(2))
    down_one = link(f1.at[mine, :], f1.at[mine, :], flip(1))
    down_rest = link(f1.at[at_slot(2), :], f1.at[at_slot(2), :], flip(1))

    for copy in loads[:4]:
        copy.wait()
    z1[mine, :] = znode[...].astype(BF16)
    nl[mine, :] = nlift[...].astype(BF16)
    z2[mine16, :] = ztop[...].astype(BF16)
    z0[...] = zleaf[...].astype(BF16)

    def enter(copies):
        pl.semaphore_wait(barrier, len(partners))
        start(copies)

    @pl.when(gives)
    def _():
        enter(give_points[:1] + proxies_two + give_points[1:] + give_detour + [give_proxy] + proxies_one + [mate_points])

    loads[4].wait()
    loads[5].wait()

    def permute(block, carry):
        rows = pl.ds(pl.multiple_of(block * wide, wide), wide)
        index = jnp.broadcast_to(order[0:1, rows].astype(F32), (128, wide)).T
        lane = lax.broadcasted_iota(jnp.int32, (wide, 128), 1).astype(F32)
        chosen = jnp.concatenate(
            [jnp.where(index == lane + 128.0 * j, 1.0, 0.0).astype(BF16) for j in range(leaf // 128)], 1)
        value = mm(chosen, charges[...])
        rhs[rows, :] = value.astype(BF16)
        return carry

    lax.fori_loop(0, PARTS, permute, 0)

    @pl.when(gives)
    def _():
        arrive(give_detour[1::2] + [give_proxy])
        start(detour_on[1::2] + [proxy_on])

    @pl.when(works)
    def _():
        enter(proxies_two + proxies_one + [mate_points])

    loads[6].wait()
    loads[7].wait()
    own = mm(rhs[...], bases[...], 0, 0).astype(BF16)
    c0[...] = own
    ut[...] = mm(own, lift[...].astype(BF16)).astype(BF16)
    start([up_near, up_cross] + mate_far)
    loads[8].wait()
    loads[9].wait()

    def augment(block, carry):
        rows = pl.ds(pl.multiple_of(block * ROWS, ROWS), ROWS)
        p = points[rows, :]
        laug[rows, 0:dim] = (p.astype(F32) * (4.0 / dim)).astype(BF16)
        laug[rows, dim:] = norm_lanes(p, -2.0 / dim, -2.0 / dim, False)
        raug[rows, 0:dim] = p
        raug[rows, dim:] = norm_lanes(p, 1.0, 1.0, True)
        return carry

    first = near[0, 0] - me
    second = near[0, 1] - me
    one = 1 - 2 * (me % 2)
    near_one = jnp.logical_or(first == one, second == one)

    def choose(a, b):
        return jnp.where(near_one, a.astype(F32), b.astype(F32)).astype(BF16)

    def tiles(rows):
        left = laug[rows, :]
        return jnp.concatenate(
            [jnp.exp(mm(left, raug[j:j + 512, :], 1, 1)).astype(BF16) for j in range(0, leaf, 512)], 1)

    def own_tile(first, last):
        def body(b, carry):
            rows = pl.ds(pl.multiple_of(b * ROWS, ROWS), ROWS)
            acc[rows, :] = mm(tiles(rows), rhs[...])
            return carry

        lax.fori_loop(first, last, body, 0)

    def carry_up():
        us[...] = (ut[at_slot(2), :].astype(F32) + rs[1].astype(F32)).astype(BF16)

    def node_level():
        total = ut[mine, :].astype(F32) + rs[0].astype(F32) + rs[2].astype(F32)
        nv[0] = total.astype(BF16)
        nv[1] = mm(total.astype(BF16), nl[...]).astype(BF16)

    def top_level():
        lifted = nv[1].astype(F32)
        for i in range(3):
            lifted = lifted + nvs[i, 1].astype(F32)
        c2[...] = lifted.astype(BF16)

    def fields_down():
        side = mm(nvs[0, 0], couple(z1s[0], z1[...]))
        for i in (1, 2):
            side = side + mm(nvs[i, 0], couple(z1s[i], z1[...]))
        field = mm(c2o[0], couple(z2o[0], z2[...]))
        for d in range(1, nodes - 1):
            field = field + mm(c2o[d], couple(z2o[d], z2[...]))
        field1 = side + mm(field.astype(BF16), nl[...], 1, 1)
        f1[mine, :] = field1.astype(BF16)

    def descend(far, final):
        f0[...] = (far() + mm(f1[...], lift[...].astype(BF16), 1, 1)).astype(BF16)

        def body(block, carry):
            rows = pl.ds(pl.multiple_of(block * ROWS, ROWS), ROWS)
            value = acc[rows, :] + mm(bases[rows, :], f0[...], 1, 1)
            if final:
                out[rows, :] = value.astype(BF16)
            else:
                acc[rows, :] = value
            return carry

        lax.fori_loop(0, blocks, body, 0)

    lax.fori_loop(0, blocks, augment, 0)

    @pl.when(gives)
    def _():
        arrive([up_cross])
        carry_up()
        start([up_two, give_rhs[0], mate_rhs])
        arrive(proxies_two)
        start(proxies_rest + [give_rhs[1]])
        own_tile(0, blocks // 2)
        arrive(proxies_one + proxies_rest + [up_near, up_two])
        start(phase_b)
        node_level()
        start(phase_two + give_rhs[2:4])
        own_tile(blocks // 2, blocks)
        arrive([mate_points, mate_rhs])
        start([give_rhs[4]])

        def mate(block, carry):
            rows = pl.ds(pl.multiple_of(block * ROWS, ROWS), ROWS)
            p = p1[rows, :]
            raug[rows, 0:dim] = p
            raug[rows, dim:] = norm_lanes(p, 1.0, 1.0, True)
            rmask[rows, :] = jnp.where(near_one, r1[rows, :].astype(F32), 0.0).astype(BF16)
            return carry

        lax.fori_loop(0, blocks, mate, 0)

        def mate_tile(b, carry):
            rows = pl.ds(pl.multiple_of(b * ROWS, ROWS), ROWS)
            acc[rows, :] += mm(tiles(rows), rmask[...])
            return carry

        lax.fori_loop(0, blocks, mate_tile, 0)
        start([give_rhs[5]])
        arrive(phase_b)
        start(top_proxies)
        arrive(phase_two)
        top_level()
        start(top_coeffs)
        arrive(top_proxies + top_coeffs)
        fields_down()
        start([down_two, down_one] + give_rhs[6:] + [give_coeff])
        arrive([down_two])
        start([down_rest])
        arrive([down_one, down_rest, back_far] + mate_far)
        descend(lambda: jnp.where(
            near_one, frecv[...].astype(F32), mm(c0x[0], couple(z0x[0], z0[...]))), False)
        for k, copy in enumerate(back_part):
            copy.wait_recv()
            out[part_rows[k], :] = (acc[part_rows[k], :] + xrecv[k].astype(F32)).astype(BF16)
        for copy in give_points + give_detour + detour_on[1::2] + [give_proxy, proxy_on, give_coeff] + give_rhs:
            copy.wait_send()

    @pl.when(works)
    def _():
        def part(tile, k, picked):
            saug[k % 2, :, 0:dim] = picked
            saug[k % 2, :, dim:] = norm_lanes(picked, 1.0, 1.0, True)
            values = jnp.concatenate(
                [jnp.exp(mm(saug[k % 2], laug[j:j + 512, :], 1, 1)).astype(BF16) for j in range(0, leaf, 512)], 1)
            tile[part_rows[k], :] = values
            return mm(values, rhs[...])

        def diagonal(k):
            dsend[k] = part(t2, k, p3[part_rows[k], :]).astype(BF16)

        def chosen(k):
            value = part(t1, k, choose(p1[part_rows[k], :], p2[part_rows[k], :]))
            racc[k % 2] = jnp.where(near_one, 0.0, value)

        def combine(k):
            xsend[k] = (racc[k % 2] + drecv[k].astype(F32)).astype(BF16)

        arrive([up_cross])
        carry_up()
        start([up_two])
        arrive([give_detour[0]])
        start([detour_on[0]])
        arrive([give_points[0], mate_points])
        start([share_points[0]])
        arrive([give_detour[2]])
        start([detour_on[2]])
        chosen(0)
        arrive([share_points[0]] + proxies_two)
        start(proxies_rest)
        diagonal(0)
        start([cross_part[0]])
        arrive([cross_part[0]])
        combine(0)
        start([back_part[0]])
        arrive([give_points[1]])
        start([share_points[1]])
        chosen(1)
        arrive([share_points[1]] + proxies_one + proxies_rest)
        start(phase_b)
        diagonal(1)
        start([cross_part[1]])
        arrive(detour_on[:2])
        start([share_points[2]])
        chosen(2)
        arrive([cross_part[1]])
        combine(1)
        start([back_part[1]])
        arrive([share_points[2], up_near, up_two] + detour_on[2:])
        start([share_points[3]])
        node_level()
        start(phase_two)
        diagonal(2)
        start([cross_part[2]])
        arrive([share_points[3]])
        chosen(3)
        arrive([cross_part[2]] + phase_b)
        combine(2)
        start([back_part[2]] + top_proxies)
        diagonal(3)
        start([cross_part[3], mate_rhs])
        arrive(phase_two + [proxy_on])
        top_level()
        fsend[...] = jnp.where(near_one, mm(c0[...], couple(z0[...], z0x[1])), 0.0).astype(BF16)
        start(top_coeffs + [back_far])
        arrive(give_rhs[:3])
        start(share_rhs[:3])
        arrive([cross_part[3]])
        combine(3)
        own_tile(0, blocks)
        arrive(top_proxies + top_coeffs + give_rhs[3:5])
        start(share_rhs[3:5])
        fields_down()
        start([down_two, down_one, back_part[3]])

        def pick_rhs(rows):
            return choose(r1[rows, :], r2[rows, :]), r3[rows, :]

        def apply(first, last):
            rows = pl.ds(first * step, (last - first) * step)
            near_rhs, far_rhs = pick_rhs(rows)
            value = mm(near_rhs, t1[rows, :], 0, 0) + mm(far_rhs, t2[rows, :], 0, 0)
            acct[...] = value if first == 0 else acct[...] + value

        def finish(j):
            rows = step_rows[j]
            arrive([give_rhs[j]])
            start([share_rhs[j]])
            acc[...] += mm(t1[rows, :], choose(r1[rows, :], r2[rows, :]), 0, 0)
            arrive([share_rhs[j]])
            acc[...] += mm(t2[rows, :], r3[rows, :], 0, 0)

        arrive(share_rhs[:4] + [mate_rhs])
        apply(0, 4)
        arrive([give_rhs[5]])
        start([share_rhs[5]])
        arrive([down_two, share_rhs[4], share_rhs[5]])
        start([down_rest])
        apply(4, 6)
        for j in range(PARTS):
            acc[part_rows[j], :] += acct[:, j * wide:(j + 1) * wide].T
        finish(6)
        finish(7)
        arrive([down_one, down_rest, give_coeff] + mate_far)
        descend(lambda: mm(choose(c0x[1], c0x[0]), couple(choose(z0x[1], z0x[0]), z0[...])), True)
        for copy in detour_on[::2] + share_points + share_rhs + cross_part + back_part + [back_far]:
            copy.wait_send()

    for copy in (proxies_two + proxies_one + proxies_rest + mate_far + phase_b + phase_two + top_proxies + top_coeffs
                 + [mate_points, mate_rhs, up_near, up_cross, up_two, down_two, down_one, down_rest]):
        copy.wait_send()


def per_device(n, near, points, charges, order, bases, lift, nlift, zleaf, znode, ztop):
    leaf, dim = points.shape
    nrhs = charges.shape[1]
    rank = lift.shape[0]
    quarter = rank // 4
    nodes = n // 16
    wide, step = leaf // PARTS, leaf // CHUNKS
    copies = 60 + 3 * PARTS + 2 * CHUNKS + 2 * nodes
    v = pltpu.VMEM
    vmem = pl.BlockSpec(memory_space=pltpu.VMEM)
    return pl.pallas_call(
        functools.partial(kernel, n),
        out_shape=jax.ShapeDtypeStruct((leaf, nrhs), BF16),
        in_specs=[pl.BlockSpec(memory_space=pltpu.HBM)] * 10,
        out_specs=vmem,
        scratch_shapes=[
            pltpu.SMEM(near.shape, near.dtype),
            v((leaf, dim), BF16), v((leaf, nrhs), BF16), v((leaf, rank), BF16), v(order.shape, order.dtype),
            v(lift.shape, F32), v(nlift.shape, F32), v(zleaf.shape, F32), v(znode.shape, F32), v(ztop.shape, F32),
            v((leaf, nrhs), BF16), v((leaf, 2 * dim), BF16), v((leaf, 2 * dim), BF16),
            v((leaf, nrhs), F32), v((nrhs, leaf), F32),
            v((leaf, dim), BF16), v((leaf, dim), BF16), v((leaf, dim), BF16),
            v((leaf, nrhs), BF16), v((leaf, nrhs), BF16), v((leaf, nrhs), BF16), v((leaf, nrhs), BF16),
            v((leaf // 2, dim), BF16), v((rank, dim), BF16),
            v((leaf, leaf), BF16), v((leaf, leaf), BF16),
            v((2, wide, 2 * dim), BF16), v((2, wide, nrhs), F32),
            v((PARTS, wide, nrhs), BF16), v((PARTS, wide, nrhs), BF16),
            v((PARTS, wide, nrhs), BF16), v((PARTS, wide, nrhs), BF16),
            v((nrhs, rank), BF16), v((nrhs, rank), BF16),
            v((nrhs, rank), BF16), v((2, nrhs, rank), BF16),
            v((rank, dim), BF16), v((2, rank, dim), BF16),
            v((nrhs, rank), BF16), v((quarter, rank), BF16), v((3, quarter, rank), BF16),
            v((rank, rank), BF16), v((rank, dim), BF16), v((3, rank, dim), BF16),
            v((rank, dim), BF16),
            v((2, quarter, rank), BF16), v((3, 2, quarter, rank), BF16),
            v((quarter, rank), BF16), v((nodes - 1, quarter, rank), BF16),
            v((nodes - 1, rank, dim), BF16), v((nrhs, rank), BF16), v((nrhs, rank), BF16),
            pltpu.SemaphoreType.DMA((copies,)), pltpu.SemaphoreType.DMA((copies,)),
            pltpu.SemaphoreType.DMA((10,)),
        ],
        compiler_params=pltpu.CompilerParams(
            collective_id=0, has_side_effects=True, vmem_limit_bytes=VMEM_MB * 1024 * 1024),
    )(*(pltpu.with_memory_space_constraint(x, pltpu.HBM) for x in (
        near, points, charges, bases, order, lift, nlift, zleaf, znode, ztop)))


def solution(mesh):
    n = mesh.shape["leaf"]

    def body(points, charges, order, near, bases, lift, nlift, zleaf, znode, ztop):
        return per_device(n, near, points, charges, order, bases, lift, nlift, zleaf, znode, ztop)

    return jax.shard_map(
        body, mesh=mesh, in_specs=(P("leaf", None),) * 10, out_specs=P("leaf", None), check_vma=False)
```

```python
import functools

import jax
import jax.numpy as jnp
from jax import lax
from jax.experimental import pallas as pl
from jax.experimental.pallas import tpu as pltpu
from jax.sharding import PartitionSpec as P

MESH = pl.DeviceIdType.MESH
F32, BF16 = jnp.float32, jnp.bfloat16
CHUNKS = 8
PARTS = 4
ROWS = 1024
VMEM_MB = 50


def mm(a, b, ca=1, cb=0):
    return lax.dot_general(a, b, (((ca,), (cb,)), ((), ())), preferred_element_type=F32)


def split3(x):
    high = x.astype(BF16).astype(F32)
    middle = (x - high).astype(BF16).astype(F32)
    return high, middle, x - high - middle


def norm_column(p):
    wide = p.astype(F32)
    return jnp.sum(wide * wide, axis=1, keepdims=True)


def norm_lanes(p, one_scale, norm_scale, norm_first):
    high, middle, low = split3(norm_column(p))
    lane = lax.broadcasted_iota(jnp.int32, (p.shape[0], 128), 1)
    first = 0 if norm_first else 3
    ones = jnp.where(lane < 6, one_scale, 0.0)
    out = jnp.where(lane == first, high * norm_scale, ones)
    out = jnp.where(lane == first + 1, middle * norm_scale, out)
    out = jnp.where(lane == first + 2, low * norm_scale, out)
    return out.astype(BF16)


def couple(left, right):
    scale = 2.0 / left.shape[1]
    wide = right.astype(F32)
    square = wide * wide
    high = square.astype(BF16)
    low = (square - high.astype(F32)).astype(BF16)
    ones = jnp.ones((8, left.shape[1]), BF16)
    right_norm = (mm(ones, high, 1, 1) + mm(ones, low, 1, 1))[0:1, :]
    return jnp.exp((2.0 * mm(left, right, 1, 1) - norm_column(left) - right_norm) * scale).astype(BF16)


def kernel(n, near_in, points_in, charges_in, bases_in, order_in, lift_in, nlift_in, zleaf_in, znode_in, ztop_in, out,
           near, points, charges, bases, order, lift, nlift, zleaf, znode, ztop, rhs, laug, raug, acc, acct,
           p1, p2, p3, r1, r2, r3, rmask, prel,
           t1, t2, saug, racc, dsend, drecv, xsend, xrecv, fsend, frecv,
           c0, c0x, z0, z0x, ut, us, rs, nl, z1, z1s, z2, nv, nvs, c2, c2o, z2o, f1, f0,
           ssem, rsem, lsem):
    me = lax.axis_index("leaf")
    leaf, dim = points.shape
    rank = lift.shape[0]
    quarter = rank // 4
    sixteenth = rank // 16
    nodes = n // 16
    slot = me % 4
    group = me // 4 % 4
    part = me % 16
    node = me // 16
    step = leaf // CHUNKS
    wide = leaf // PARTS
    half = PARTS // 2
    blocks = leaf // ROWS
    gives = (me // 2 + me // 4 + me // 8) % 2 == 0
    works = (me // 2 + me // 4 + me // 8) % 2 == 1

    def flip(bits):
        where = me
        for bit in (1, 2, 4, 8):
            if bits & bit:
                where = where + bit - 2 * bit * (me // bit % 2)
        return where

    def flip_slot(bits):
        return flip(bits) % 4

    others = [(node + d) % nodes * 16 + part for d in range(1, nodes)]

    barrier = pltpu.get_barrier_semaphore()
    partners = [flip(b) for b in (1, 2, 4, 6, 8, 10, 12)] + others
    for other in partners:
        pl.semaphore_signal(barrier, inc=1, device_id=(other,), device_id_type=MESH)

    loads = [pltpu.make_async_copy(a, b, lsem.at[i]) for i, (a, b) in enumerate((
        (znode_in, znode), (nlift_in, nlift), (ztop_in, ztop), (zleaf_in, zleaf), (order_in, order), (charges_in, charges),
        (bases_in, bases), (lift_in, lift), (points_in, points), (near_in, near)))]
    for copy in loads:
        copy.start()
    def start(copies):
        for copy in copies:
            copy.start()

    def arrive(copies):
        for copy in copies:
            copy.wait_recv()

    count = [0]

    def link(src, dst, device):
        i = count[0]
        count[0] += 1
        return pltpu.make_async_remote_copy(
            src_ref=src, dst_ref=dst, send_sem=ssem.at[i], recv_sem=rsem.at[i],
            device_id=(device,), device_id_type=MESH)

    def at_slot(bits):
        where = flip_slot(bits) if bits else slot
        return pl.ds(pl.multiple_of(where * quarter, quarter), quarter)

    mine = at_slot(0)
    mine16 = pl.ds(pl.multiple_of(part * sixteenth, sixteenth), sixteenth)
    far16 = pl.ds(pl.multiple_of(flip(2) % 16 * sixteenth, sixteenth), sixteenth)
    mine64 = pl.ds(pl.multiple_of(group * quarter, quarter), quarter)
    part_rows = [pl.ds(k * wide, wide) for k in range(PARTS)]
    step_rows = [pl.ds(j * step, step) for j in range(CHUNKS)]

    give_points = [link(points_in.at[r, :], p2.at[r, :], flip(2)) for r in part_rows[:half]]
    detour_rows = [(pl.ds(half * wide + q * step, step), pl.ds(q * step, step)) for q in range(CHUNKS // 2)]
    give_detour = [link(points_in.at[r, :], prel.at[at, :], flip((4, 10)[q % 2]))
                   for q, (r, at) in enumerate(detour_rows)]
    detour_on = [link(prel.at[at, :], p2.at[r, :], flip((6, 8)[q % 2])) for q, (r, at) in enumerate(detour_rows)]
    give_proxy = link(z0, z0x.at[1], flip(2))
    give_coeff = link(c0, c0x.at[1], flip(2))
    give_rhs = [link(rhs.at[r, :], r2.at[r, :], flip(2)) for r in step_rows]
    share_points = [link(p2.at[r, :], p3.at[r, :], flip(1)) for r in part_rows]
    share_rhs = [link(r2.at[r, :], r3.at[r, :], flip(1)) for r in step_rows]
    cross_part = [link(dsend.at[k], drecv.at[k], flip(1)) for k in range(PARTS)]
    back_part = [link(xsend.at[k], xrecv.at[k], flip(2)) for k in range(PARTS)]
    back_far = link(fsend, frecv, flip(2))
    proxies_two = [link(z1.at[mine, :], z1.at[mine, :], flip(2)),
                   link(nl.at[mine, :], nl.at[mine, :], flip(2)),
                   link(z2.at[mine16, :], z2.at[mine16, :], flip(2))]
    proxies_one = [link(z1.at[mine, :], z1.at[mine, :], flip(1)),
                   link(nl.at[mine, :], nl.at[mine, :], flip(1)),
                   link(z2.at[mine16, :], z2.at[mine16, :], flip(1))]
    proxies_rest = [link(z1.at[at_slot(2), :], z1.at[at_slot(2), :], flip(1)),
                    link(nl.at[at_slot(2), :], nl.at[at_slot(2), :], flip(1)),
                    link(z2.at[far16, :], z2.at[far16, :], flip(1))]
    mate_points = link(points_in, p1, flip(1))
    mate_far = [link(c0, c0x.at[0], flip(1)), link(z0, z0x.at[0], flip(1))]
    up_near = link(ut.at[at_slot(1), :], rs.at[0], flip(1))
    up_cross = link(ut.at[at_slot(3), :], rs.at[1], flip(1))
    mate_rhs = link(rhs, r1, flip(1))
    up_two = link(us, rs.at[2], flip(2))
    phase_b = []
    for i, b in enumerate((4, 8, 12)):
        phase_b.append(link(z1, z1s.at[i], flip(b)))
        phase_b.append(link(z2.at[mine64, :], z2.at[mine64, :], flip(b)))
    phase_two = [link(nv, nvs.at[i], flip(b)) for i, b in enumerate((4, 8, 12))]
    top_proxies = [link(z2, z2o.at[d], other) for d, other in enumerate(others)]
    top_coeffs = [link(c2, c2o.at[d], other) for d, other in enumerate(others)]
    down_two = link(f1.at[mine, :], f1.at[mine, :], flip(2))
    down_one = link(f1.at[mine, :], f1.at[mine, :], flip(1))
    down_rest = link(f1.at[at_slot(2), :], f1.at[at_slot(2), :], flip(1))

    for copy in loads[:4]:
        copy.wait()
    z1[mine, :] = znode[...].astype(BF16)
    nl[mine, :] = nlift[...].astype(BF16)
    z2[mine16, :] = ztop[...].astype(BF16)
    z0[...] = zleaf[...].astype(BF16)

    def enter(copies):
        pl.semaphore_wait(barrier, len(partners))
        start(copies)

    @pl.when(gives)
    def _():
        enter(give_points[:1] + proxies_two + give_points[1:] + give_detour + [give_proxy] + proxies_one + [mate_points])

    loads[4].wait()
    loads[5].wait()

    def permute(block, carry):
        rows = pl.ds(pl.multiple_of(block * wide, wide), wide)
        index = jnp.broadcast_to(order[0:1, rows].astype(F32), (128, wide)).T
        lane = lax.broadcasted_iota(jnp.int32, (wide, 128), 1).astype(F32)
        chosen = jnp.concatenate(
            [jnp.where(index == lane + 128.0 * j, 1.0, 0.0).astype(BF16) for j in range(leaf // 128)], 1)
        value = mm(chosen, charges[...])
        rhs[rows, :] = value.astype(BF16)
        return carry

    lax.fori_loop(0, PARTS, permute, 0)

    @pl.when(works)
    def _():
        enter(proxies_two + proxies_one + [mate_points])

    loads[6].wait()
    loads[7].wait()
    own = mm(rhs[...], bases[...], 0, 0).astype(BF16)
    c0[...] = own
    ut[...] = mm(own, lift[...].astype(BF16)).astype(BF16)
    start([up_near, up_cross] + mate_far)
    loads[8].wait()
    loads[9].wait()

    def augment(block, carry):
        rows = pl.ds(pl.multiple_of(block * ROWS, ROWS), ROWS)
        p = points[rows, :]
        laug[rows, 0:dim] = (p.astype(F32) * (4.0 / dim)).astype(BF16)
        laug[rows, dim:] = norm_lanes(p, -2.0 / dim, -2.0 / dim, False)
        raug[rows, 0:dim] = p
        raug[rows, dim:] = norm_lanes(p, 1.0, 1.0, True)
        return carry

    first = near[0, 0] - me
    second = near[0, 1] - me
    one = 1 - 2 * (me % 2)
    near_one = jnp.logical_or(first == one, second == one)

    def choose(a, b):
        return jnp.where(near_one, a.astype(F32), b.astype(F32)).astype(BF16)

    def tiles(rows):
        left = laug[rows, :]
        return jnp.concatenate(
            [jnp.exp(mm(left, raug[j:j + 512, :], 1, 1)).astype(BF16) for j in range(0, leaf, 512)], 1)

    def own_tile(first, last):
        def body(b, carry):
            rows = pl.ds(pl.multiple_of(b * ROWS, ROWS), ROWS)
            acc[rows, :] = mm(tiles(rows), rhs[...])
            return carry

        lax.fori_loop(first, last, body, 0)

    def carry_up():
        us[...] = (ut[at_slot(2), :].astype(F32) + rs[1].astype(F32)).astype(BF16)

    def node_level():
        total = ut[mine, :].astype(F32) + rs[0].astype(F32) + rs[2].astype(F32)
        nv[0] = total.astype(BF16)
        nv[1] = mm(total.astype(BF16), nl[...]).astype(BF16)

    def top_level():
        lifted = nv[1].astype(F32)
        for i in range(3):
            lifted = lifted + nvs[i, 1].astype(F32)
        c2[...] = lifted.astype(BF16)

    def fields_down():
        side = mm(nvs[0, 0], couple(z1s[0], z1[...]))
        for i in (1, 2):
            side = side + mm(nvs[i, 0], couple(z1s[i], z1[...]))
        field = mm(c2o[0], couple(z2o[0], z2[...]))
        for d in range(1, nodes - 1):
            field = field + mm(c2o[d], couple(z2o[d], z2[...]))
        field1 = side + mm(field.astype(BF16), nl[...], 1, 1)
        f1[mine, :] = field1.astype(BF16)

    def descend(far, final):
        f0[...] = (far() + mm(f1[...], lift[...].astype(BF16), 1, 1)).astype(BF16)

        def body(block, carry):
            rows = pl.ds(pl.multiple_of(block * ROWS, ROWS), ROWS)
            value = acc[rows, :] + mm(bases[rows, :], f0[...], 1, 1)
            if final:
                out[rows, :] = value.astype(BF16)
            else:
                acc[rows, :] = value
            return carry

        lax.fori_loop(0, blocks, body, 0)

    lax.fori_loop(0, blocks, augment, 0)

    @pl.when(gives)
    def _():
        arrive([up_cross])
        carry_up()
        start([up_two, give_rhs[0], mate_rhs])
        arrive(give_detour[1::2])
        start(detour_on[1::2])
        arrive(proxies_two)
        start(proxies_rest + [give_rhs[1]])
        own_tile(0, blocks // 2)
        arrive(proxies_one + proxies_rest + [up_near, up_two])
        start(phase_b)
        node_level()
        start(phase_two + give_rhs[2:4])
        own_tile(blocks // 2, blocks)
        arrive([mate_points, mate_rhs])
        start([give_rhs[4]])

        def mate(block, carry):
            rows = pl.ds(pl.multiple_of(block * ROWS, ROWS), ROWS)
            p = p1[rows, :]
            raug[rows, 0:dim] = p
            raug[rows, dim:] = norm_lanes(p, 1.0, 1.0, True)
            rmask[rows, :] = jnp.where(near_one, r1[rows, :].astype(F32), 0.0).astype(BF16)
            return carry

        lax.fori_loop(0, blocks, mate, 0)

        def mate_tile(b, carry):
            rows = pl.ds(pl.multiple_of(b * ROWS, ROWS), ROWS)
            acc[rows, :] += mm(tiles(rows), rmask[...])
            return carry

        lax.fori_loop(0, blocks, mate_tile, 0)
        start(give_rhs[5:7])
        arrive(phase_b)
        start(top_proxies)
        arrive(phase_two)
        top_level()
        start(top_coeffs)
        arrive(top_proxies + top_coeffs)
        fields_down()
        start([down_two, down_one, give_rhs[7], give_coeff])
        arrive([down_two])
        start([down_rest])
        arrive([down_one, down_rest, back_far] + mate_far)
        descend(lambda: jnp.where(
            near_one, frecv[...].astype(F32), mm(c0x[0], couple(z0x[0], z0[...]))), False)
        for k, copy in enumerate(back_part):
            copy.wait_recv()
            out[part_rows[k], :] = (acc[part_rows[k], :] + xrecv[k].astype(F32)).astype(BF16)
        for copy in give_points + give_detour + detour_on[1::2] + [give_proxy, give_coeff] + give_rhs:
            copy.wait_send()

    @pl.when(works)
    def _():
        def part(tile, k, picked):
            saug[k % 2, :, 0:dim] = picked
            saug[k % 2, :, dim:] = norm_lanes(picked, 1.0, 1.0, True)
            values = jnp.concatenate(
                [jnp.exp(mm(saug[k % 2], laug[j:j + 512, :], 1, 1)).astype(BF16) for j in range(0, leaf, 512)], 1)
            tile[part_rows[k], :] = values
            return mm(values, rhs[...])

        def diagonal(k):
            dsend[k] = part(t2, k, p3[part_rows[k], :]).astype(BF16)

        def chosen(k):
            value = part(t1, k, choose(p1[part_rows[k], :], p2[part_rows[k], :]))
            racc[k % 2] = jnp.where(near_one, 0.0, value)

        def combine(k):
            xsend[k] = (racc[k % 2] + drecv[k].astype(F32)).astype(BF16)

        arrive([up_cross])
        carry_up()
        start([up_two])
        arrive([give_detour[0]])
        start([detour_on[0]])
        arrive([give_points[0], mate_points])
        start([share_points[0]])
        arrive([give_detour[2]])
        start([detour_on[2]])
        chosen(0)
        arrive([share_points[0]] + proxies_two)
        start(proxies_rest)
        diagonal(0)
        start([cross_part[0]])
        arrive([cross_part[0]])
        combine(0)
        start([back_part[0]])
        arrive([give_points[1]])
        start([share_points[1]])
        chosen(1)
        arrive([share_points[1]] + proxies_one + proxies_rest)
        start(phase_b)
        diagonal(1)
        start([cross_part[1]])
        arrive(detour_on[:2])
        start([share_points[2]])
        chosen(2)
        arrive([cross_part[1]])
        combine(1)
        start([back_part[1]])
        arrive([share_points[2], up_near, up_two] + detour_on[2:])
        start([share_points[3]])
        node_level()
        start(phase_two)
        diagonal(2)
        start([cross_part[2]])
        arrive([share_points[3]])
        chosen(3)
        arrive([cross_part[2]] + phase_b)
        combine(2)
        start([back_part[2]] + top_proxies)
        diagonal(3)
        start([cross_part[3], mate_rhs])
        arrive(phase_two + [give_proxy])
        top_level()
        fsend[...] = jnp.where(near_one, mm(c0[...], couple(z0[...], z0x[1])), 0.0).astype(BF16)
        start(top_coeffs + [back_far])
        arrive(give_rhs[:3])
        start(share_rhs[:3])
        arrive([cross_part[3]])
        combine(3)
        own_tile(0, blocks)
        arrive(top_proxies + top_coeffs + give_rhs[3:5])
        start(share_rhs[3:5])
        fields_down()
        start([down_two, down_one, back_part[3]])

        def pick_rhs(rows):
            return choose(r1[rows, :], r2[rows, :]), r3[rows, :]

        def apply(first, last):
            rows = pl.ds(first * step, (last - first) * step)
            near_rhs, far_rhs = pick_rhs(rows)
            value = mm(near_rhs, t1[rows, :], 0, 0) + mm(far_rhs, t2[rows, :], 0, 0)
            acct[...] = value if first == 0 else acct[...] + value

        def finish(j):
            rows = step_rows[j]
            arrive([give_rhs[j]])
            start([share_rhs[j]])
            acc[...] += mm(t1[rows, :], choose(r1[rows, :], r2[rows, :]), 0, 0)
            arrive([share_rhs[j]])
            acc[...] += mm(t2[rows, :], r3[rows, :], 0, 0)

        arrive(share_rhs[:4] + [mate_rhs])
        apply(0, 4)
        arrive([give_rhs[5]])
        start([share_rhs[5]])
        arrive(share_rhs[4:6])
        apply(4, 6)
        arrive([down_two])
        start([down_rest])
        for j in range(PARTS):
            acc[part_rows[j], :] += acct[:, j * wide:(j + 1) * wide].T
        finish(6)
        finish(7)
        arrive([down_one, down_rest, give_coeff] + mate_far)
        descend(lambda: mm(choose(c0x[1], c0x[0]), couple(choose(z0x[1], z0x[0]), z0[...])), True)
        for copy in detour_on[::2] + share_points + share_rhs + cross_part + back_part + [back_far]:
            copy.wait_send()

    for copy in (proxies_two + proxies_one + proxies_rest + mate_far + phase_b + phase_two + top_proxies + top_coeffs
                 + [mate_points, mate_rhs, up_near, up_cross, up_two, down_two, down_one, down_rest]):
        copy.wait_send()


def per_device(n, near, points, charges, order, bases, lift, nlift, zleaf, znode, ztop):
    leaf, dim = points.shape
    nrhs = charges.shape[1]
    rank = lift.shape[0]
    quarter = rank // 4
    nodes = n // 16
    wide, step = leaf // PARTS, leaf // CHUNKS
    copies = 60 + 3 * PARTS + 2 * CHUNKS + 2 * nodes
    v = pltpu.VMEM
    vmem = pl.BlockSpec(memory_space=pltpu.VMEM)
    return pl.pallas_call(
        functools.partial(kernel, n),
        out_shape=jax.ShapeDtypeStruct((leaf, nrhs), BF16),
        in_specs=[pl.BlockSpec(memory_space=pltpu.HBM)] * 10,
        out_specs=vmem,
        scratch_shapes=[
            pltpu.SMEM(near.shape, near.dtype),
            v((leaf, dim), BF16), v((leaf, nrhs), BF16), v((leaf, rank), BF16), v(order.shape, order.dtype),
            v(lift.shape, F32), v(nlift.shape, F32), v(zleaf.shape, F32), v(znode.shape, F32), v(ztop.shape, F32),
            v((leaf, nrhs), BF16), v((leaf, 2 * dim), BF16), v((leaf, 2 * dim), BF16),
            v((leaf, nrhs), F32), v((nrhs, leaf), F32),
            v((leaf, dim), BF16), v((leaf, dim), BF16), v((leaf, dim), BF16),
            v((leaf, nrhs), BF16), v((leaf, nrhs), BF16), v((leaf, nrhs), BF16), v((leaf, nrhs), BF16),
            v((leaf // 2, dim), BF16),
            v((leaf, leaf), BF16), v((leaf, leaf), BF16),
            v((2, wide, 2 * dim), BF16), v((2, wide, nrhs), F32),
            v((PARTS, wide, nrhs), BF16), v((PARTS, wide, nrhs), BF16),
            v((PARTS, wide, nrhs), BF16), v((PARTS, wide, nrhs), BF16),
            v((nrhs, rank), BF16), v((nrhs, rank), BF16),
            v((nrhs, rank), BF16), v((2, nrhs, rank), BF16),
            v((rank, dim), BF16), v((2, rank, dim), BF16),
            v((nrhs, rank), BF16), v((quarter, rank), BF16), v((3, quarter, rank), BF16),
            v((rank, rank), BF16), v((rank, dim), BF16), v((3, rank, dim), BF16),
            v((rank, dim), BF16),
            v((2, quarter, rank), BF16), v((3, 2, quarter, rank), BF16),
            v((quarter, rank), BF16), v((nodes - 1, quarter, rank), BF16),
            v((nodes - 1, rank, dim), BF16), v((nrhs, rank), BF16), v((nrhs, rank), BF16),
            pltpu.SemaphoreType.DMA((copies,)), pltpu.SemaphoreType.DMA((copies,)),
            pltpu.SemaphoreType.DMA((10,)),
        ],
        compiler_params=pltpu.CompilerParams(
            collective_id=0, has_side_effects=True, vmem_limit_bytes=VMEM_MB * 1024 * 1024),
    )(*(pltpu.with_memory_space_constraint(x, pltpu.HBM) for x in (
        near, points, charges, bases, order, lift, nlift, zleaf, znode, ztop)))


def solution(mesh):
    n = mesh.shape["leaf"]

    def body(points, charges, order, near, bases, lift, nlift, zleaf, znode, ztop):
        return per_device(n, near, points, charges, order, bases, lift, nlift, zleaf, znode, ztop)

    return jax.shard_map(
        body, mesh=mesh, in_specs=(P("leaf", None),) * 10, out_specs=P("leaf", None), check_vma=False)
```
